32 devices in a mesh: gx: 2 (over x), gy: 16 (over z, y, core).
Axes of the slice: x: 2, y: 2, z: 4, core: 2. Of those that a mesh axis runs over, the one named last changes fastest.
Arguments:
- concentration: float32 [64, 256, 256], P('gx', 'gy'), may hold values from 0.1 to 4
- face_conductance: float32 [64, 256, 256], P('gx', 'gy'), may hold values from 3 to 1000
- release: float32 [64, 256, 256], P('gx', 'gy'), may hold values from 0.1 to 1
- trap_rate: float32 [64, 256, 256], P('gx', 'gy'), may hold values from 0.5 to 2
Outputs:
- final_concentration: float32 [64, 256, 256], P('gx', 'gy')
The draws below stay inside these ranges and needn't reach their ends.
All inputs are finite; a program needn't handle non-finite values.
Results may differ from the reference program's by a relative error of at most 0.0003.
Values sent between devices are 32-bit elements; how exact they have to be, the bound alone decides.
A program may use at most 64 MiB of HBM per device.

```python
import math
import jax
import jax.numpy as jnp
from jax import lax

CZ = 256
STEPS = 2
SUBSTEPS = 4
NX = 64
NY = 256


def shard_levels(key, extent, pieces, smallest, high):
    factor_of = 1.0
    for dim, parts in pieces:
        draws = jax.random.uniform(jax.random.fold_in(jax.random.fold_in(key, 6), dim), (parts,), jnp.float32, smallest / len(pieces), high / len(pieces))
        factor_of = factor_of * jnp.repeat(jnp.exp(draws), extent[dim] // parts).reshape((-1,) + (1,) * (len(extent) - 1 - dim))
    return factor_of


def setup_inputs(seed: int = 0) -> dict:
    splits = jax.random.split(jax.random.key(seed), 5)
    return {
        "concentration": jnp.clip(jnp.exp(math.log(4.0) - 3.6888794 * jax.random.uniform(splits[0], (NX, NY, CZ), jnp.float32) ** shard_levels(splits[0], (NX, NY, CZ), ((0, 2), (1, 16)), -0.2, 0.2)), 0.1, 4.0),
        "face_conductance": jnp.clip(jnp.exp(math.log(1000.0) - 5.809143 * jax.random.uniform(splits[1], (NX, NY, CZ), jnp.float32) ** shard_levels(splits[1], (NX, NY, CZ), ((0, 2), (1, 16)), -0.2, 0.2)), 3.0, 1000.0),
        "release": jnp.clip(jnp.exp(math.log(1.0) - 2.3025851 * jax.random.uniform(splits[2], (NX, NY, CZ), jnp.float32) ** shard_levels(splits[2], (NX, NY, CZ), ((0, 2), (1, 16)), -0.2, 0.2)), 0.1, 1.0),
        "trap_rate": jnp.clip(jnp.exp(math.log(2.0) - 1.3862944 * jax.random.uniform(splits[3], (NX, NY, CZ), jnp.float32) ** shard_levels(splits[3], (NX, NY, CZ), ((0, 2), (1, 16)), -0.2, 0.2)), 0.5, 2.0),
    }


y_weight = 0.32
z_weight = 0.16
time_step = 0.25


def thomas(lower, middle, upper, right):
    def forward(carry, row):
        factor_prev, value_prev = carry
        below_row, main_row, above_row, right_row = row
        divisor = main_row - below_row * factor_prev
        factor = above_row / divisor
        scaled = (right_row - below_row[None] * value_prev) / divisor[None]
        return (factor, scaled), (factor, scaled)

    start = (jnp.zeros_like(middle[0]), jnp.zeros_like(right[0]))
    unused, (factors, scaled) = lax.scan(forward, start, (lower, middle, upper, right))

    def backward(following, row):
        factor, value = row
        current = value - factor[None] * following
        return current, current

    unused, values = lax.scan(backward, jnp.zeros_like(right[0]), (factors, scaled), reverse=True)
    return values


def advance(center, below, above, release, trap_rate):
    left = jnp.concatenate([center[:, :, :1], center[:, :, :-1]], axis=2)
    right = jnp.concatenate([center[:, :, 1:], center[:, :, -1:]], axis=2)
    square = center * center
    reaction = release - trap_rate * square / (1.0 + square)
    return center + y_weight * (above + below - 2.0 * center) + z_weight * (left + right - 2.0 * center) + time_step * reaction


def line_solve(field, face_conductance):
    rows_x = field.shape[0]
    inside = (jnp.arange(rows_x) < rows_x - 1)[:, None, None]
    faces_used = jnp.where(inside, face_conductance, jnp.float32(0.0))
    blank = jnp.zeros_like(faces_used[:1])
    before = jnp.concatenate([blank, faces_used[:-1]], axis=0)
    return thomas(-before, 1.0 + before + faces_used, -faces_used, field[:, None])[:, 0]


def reference(concentration, face_conductance, release, trap_rate):
    field = concentration
    for step in range(STEPS):
        field = line_solve(field, face_conductance)
        for substep in range(SUBSTEPS):
            padded = jnp.pad(field, ((0, 0), (1, 1), (0, 0)))
            field = advance(field, padded[:, :-2], padded[:, 2:], release, trap_rate)
    return field
```

```python
import jax
import jax.numpy as jnp
from jax import lax
from jax.experimental import pallas as pl
from jax.experimental.pallas import tpu as pltpu
from jax.sharding import PartitionSpec as P

STEPS = 2
SUBSTEPS = 4


y_weight = 0.32
z_weight = 0.16
time_step = 0.25


def shifted(value, axis, by):
    peers = lax.axis_size(axis)
    pairs = [(i, i + by) for i in range(peers) if 0 <= i + by < peers]
    return lax.ppermute(value, axis, pairs)


def extended_2(block, sides, width):
    for axis, dim in sides:
        count = lax.axis_size(axis)
        forward = [(i, i + 1) for i in range(count - 1)]
        backward = [(target, source) for source, target in forward]
        low = lax.ppermute(
            lax.slice_in_dim(block, block.shape[dim] - width, None, axis=dim), axis, forward
        )
        high = lax.ppermute(lax.slice_in_dim(block, 0, width, axis=dim), axis, backward)
        block = jnp.concatenate([low, block, high], axis=dim)
    return block


def thomas(lower, middle, upper, right):

    def forward(carry, row):
        factor_prev, value_prev = carry
        below_row, main_row, above_row, right_row = row
        divisor = main_row - below_row * factor_prev
        factor = above_row / divisor
        scaled = (right_row - below_row[None] * value_prev) / divisor[None]
        return ((factor, scaled), (factor, scaled))

    start = (jnp.zeros_like(middle[0]), jnp.zeros_like(right[0]))
    unused, (factors, scaled) = lax.scan(forward, start, (lower, middle, upper, right))

    def backward(following, row):
        factor, value = row
        current = value - factor[None] * following
        return (current, current)

    unused, values = lax.scan(backward, jnp.zeros_like(right[0]), (factors, scaled), reverse=True)
    return values


def advance(center, below, above, release, trap_rate):
    left = jnp.concatenate([center[:, :, :1], center[:, :, :-1]], axis=2)
    right = jnp.concatenate([center[:, :, 1:], center[:, :, -1:]], axis=2)
    square = center * center
    reaction = release - trap_rate * square / (1.0 + square)
    return (
        center
        + y_weight * (above + below - 2.0 * center)
        + z_weight * (left + right - 2.0 * center)
        + time_step * reaction
    )


def line_section(field, faces_used):
    rows_x = field.shape[0]
    blank = jnp.zeros_like(faces_used[:1])
    lower = jnp.concatenate([blank, -faces_used[1 : rows_x - 1]], axis=0)
    upper = jnp.concatenate([-faces_used[1 : rows_x - 1], blank], axis=0)
    middle = 1.0 + faces_used[:-1] + faces_used[1:]
    row_index = jnp.arange(rows_x - 1)[:, None, None]
    first_unit = jnp.where(row_index == 0, faces_used[0:1], jnp.float32(0.0))
    last_unit = jnp.where(
        row_index == rows_x - 2, faces_used[rows_x - 1 : rows_x], jnp.float32(0.0)
    )
    right = jnp.stack([field[1:], first_unit, last_unit], axis=1)
    solved = thomas(lower, middle, upper, right)
    inner = solved[:, 0]
    left_part = solved[:, 1]
    right_part = solved[:, 2]
    edge = jnp.stack([faces_used[-1], inner[-1], left_part[-1], right_part[-1]])
    came = shifted(edge, "gx", 1)
    prior_face = came[0]
    own_face = faces_used[0]
    coef_lower = -prior_face * came[2]
    coef_main = 1.0 + prior_face + own_face - prior_face * came[3] - own_face * left_part[0]
    coef_upper = -own_face * right_part[0]
    coef_right = field[0] + prior_face * came[1] + own_face * inner[0]
    system = jnp.stack([coef_lower, coef_main, coef_upper, coef_right])[:, None]
    whole = lax.all_gather(system, "gx", axis=1, tiled=True)
    firsts = thomas(whole[0], whole[1], whole[2], whole[3][:, None])[:, 0]
    position = lax.axis_index("gx")
    count = lax.axis_size("gx")
    first = lax.dynamic_index_in_dim(firsts, position, 0, keepdims=False)
    following = lax.dynamic_index_in_dim(
        firsts, jnp.minimum(position + 1, count - 1), 0, keepdims=False
    )
    rest = inner + first[None] * left_part + following[None] * right_part
    return jnp.concatenate([first[None], rest], axis=0)


def local(concentration, face_conductance, release, trap_rate):
    rows_x = concentration.shape[0]
    rows_y = concentration.shape[1]
    is_last = lax.axis_index("gx") == lax.axis_size("gx") - 1
    inside = jnp.logical_or(
        jnp.arange(rows_x)[:, None, None] < rows_x - 1, jnp.logical_not(is_last)
    )
    faces_used = jnp.where(inside, face_conductance, jnp.float32(0.0))
    field = concentration
    margin = SUBSTEPS
    rates = extended_2(jnp.stack([release, trap_rate]), (("gy", 2),), margin)
    global_rows = lax.axis_index("gy") * rows_y - margin + jnp.arange(rows_y + 2 * margin)
    valid = jnp.logical_and(global_rows >= 0, global_rows < lax.axis_size("gy") * rows_y)
    for step in range(STEPS):
        field = line_section(field, faces_used)
        extended = extended_2(field, (("gy", 1),), margin)
        for substep in range(SUBSTEPS):
            span = extended.shape[1] - 2
            offset = substep + 1
            source_part = rates[0][:, offset : offset + span]
            trap_part = rates[1][:, offset : offset + span]
            keeping = valid[offset : offset + span][None, :, None]
            updated = advance(
                extended[:, 1:-1], extended[:, :-2], extended[:, 2:], source_part, trap_part
            )
            extended = jnp.where(keeping, updated, jnp.float32(0.0))
        field = extended
    return field


SUB = 8
LANES = 128
CHUNKS = 4
MESH = pl.DeviceIdType.MESH


def inverse(value):
    return 1.0 / value


def kernel(
    c_hbm, f_hbm, rel_hbm, trap_hbm, out,
    c_in, f_in, rel_in, trap_in, factor, scale, partial, field,
    rate_out, rate_got, halo_out, halo_got, edge_out, edge_got,
    load_sem, edge_send, edge_recv, rate_send, rate_recv, halo_send, halo_recv,
):
    planes, rows, depth = c_in.shape
    groups = rows // SUB
    blocks = depth // LANES
    pairs = planes // 2
    per_chunk = pairs // CHUNKS
    side = lax.axis_index("gx")
    spot = lax.axis_index("gy")
    count = lax.axis_size("gy")
    has_prev = spot > 0
    has_next = spot < count - 1
    partner = {"gx": 1 - side}
    to_next = {"gy": jnp.minimum(spot + 1, count - 1)}
    to_prev = {"gy": jnp.maximum(spot - 1, 0)}

    def plane_of(i):
        return i + side * (planes - 1 - 2 * i)

    loads = [
        pltpu.make_async_copy(src, dst, load_sem.at[n])
        for n, (src, dst) in enumerate(
            [(rel_hbm, rel_in), (trap_hbm, trap_in), (f_hbm, f_in), (c_hbm, c_in)]
        )
    ]
    for load in loads:
        load.start()

    barrier = pltpu.get_barrier_semaphore()
    pl.semaphore_signal(barrier, inc=1, device_id=partner, device_id_type=MESH)

    @pl.when(has_next)
    def _():
        pl.semaphore_signal(barrier, inc=1, device_id=to_next, device_id_type=MESH)

    @pl.when(has_prev)
    def _():
        pl.semaphore_signal(barrier, inc=1, device_id=to_prev, device_id_type=MESH)

    sub_index = lax.broadcasted_iota(jnp.int32, (SUB, depth), 0)
    low_half = sub_index < SUB // 2

    def both(first, second):
        return jnp.where(low_half, first, second)

    def turned(value):
        return pltpu.roll(value, SUB // 2, axis=0)

    def remote(src, dst, send, recv, target):
        return pltpu.make_async_remote_copy(
            src_ref=src, dst_ref=dst, send_sem=send, recv_sem=recv,
            device_id=target, device_id_type=MESH,
        )

    rate_copies = [
        remote(rate_out.at[n], rate_got.at[n], rate_send.at[n], rate_recv.at[n], target)
        for n, target in enumerate((to_next, to_prev))
    ]

    def halo_copy(step, chunk, n):
        part = pl.ds(chunk * per_chunk, per_chunk)
        return remote(
            halo_out.at[step, n, part], halo_got.at[step, n, part],
            halo_send.at[step, chunk, n], halo_recv.at[step, chunk, n],
            (to_next, to_prev)[n],
        )

    def start_two(first, second):
        @pl.when(has_next)
        def _():
            first.start()

        @pl.when(has_prev)
        def _():
            second.start()

    def got_two(first, second):
        @pl.when(has_prev)
        def _():
            first.wait_recv()

        @pl.when(has_next)
        def _():
            second.wait_recv()

    def sent_two(first, second):
        @pl.when(has_next)
        def _():
            first.wait_send()

        @pl.when(has_prev)
        def _():
            second.wait_send()

    loads[0].wait()
    loads[1].wait()

    def prepare(i, carry):
        x = plane_of(i)
        trap = time_step * trap_in[x]
        base = time_step * rel_in[x] - trap
        trap_in[x] = trap
        rel_in[x] = base
        rate_out[0, i] = both(turned(trap[rows - SUB:]), base[rows - SUB:])
        rate_out[1, i] = both(base[:SUB], turned(trap[:SUB]))
        return carry

    lax.fori_loop(0, planes, prepare, 0, unroll=4)

    pl.semaphore_wait(barrier, 1 + has_prev.astype(jnp.int32) + has_next.astype(jnp.int32))
    start_two(*rate_copies)

    loads[2].wait()
    loads[3].wait()

    second_edge = remote(
        edge_out.at[3], edge_got.at[3], edge_send.at[1], edge_recv.at[1], partner
    )
    first_edge = remote(
        edge_out.at[pl.ds(0, 3)], edge_got.at[pl.ds(0, 3)],
        edge_send.at[0], edge_recv.at[0], partner,
    )

    lane = lax.broadcasted_iota(jnp.int32, (SUB, LANES), 1)
    sub = lax.broadcasted_iota(jnp.int32, (SUB, LANES), 0)
    lane_first, lane_last = lane == 0, lane == LANES - 1
    sub_first, sub_last = sub == 0, sub == SUB - 1
    present = jnp.where(
        sub < SUB // 2, has_next.astype(jnp.int32), has_prev.astype(jnp.int32)
    ) > 0

    def substep(now, base, trap, with_halo):
        up = [[pltpu.roll(v, 1, axis=0) for v in g] for g in now]
        down = [[pltpu.roll(v, SUB - 1, axis=0) for v in g] for g in now]
        total = groups + 1
        made = []
        for g in range(total if with_halo else groups):
            ahead, behind = (g + 1) % total, (g - 1) % total
            right = [pltpu.roll(v, 1, axis=1) for v in now[g]]
            left = [pltpu.roll(v, LANES - 1, axis=1) for v in now[g]]
            row = []
            for b in range(blocks):
                c = now[g][b]
                above = jnp.where(sub_first, up[behind][b], up[g][b])
                below = jnp.where(sub_last, down[ahead][b], down[g][b])
                lower = jnp.where(lane_first, right[b - 1] if b > 0 else c, right[b])
                upper = jnp.where(lane_last, left[b + 1] if b < blocks - 1 else c, left[b])
                value = (
                    (1.0 - 2.0 * y_weight - 2.0 * z_weight) * c
                    + y_weight * (above + below)
                    + z_weight * (lower + upper)
                    + (base[g][b] + trap[g][b] * inverse(1.0 + c * c))
                )
                if g == groups:
                    value = jnp.where(present, value, 0.0)
                row.append(value)
            made.append(row)
        return made

    def cut(value):
        return [value[:, b * LANES:(b + 1) * LANES] for b in range(blocks)]

    def whole(ref, x):
        return [
            [ref[x, g * SUB:(g + 1) * SUB, b * LANES:(b + 1) * LANES] for b in range(blocks)]
            for g in range(groups)
        ]

    for step in range(STEPS):
        source = (lambda i: c_in[plane_of(i)]) if step == 0 else (lambda i: field[i])
        right = source(0)
        if step == 0:
            main = jnp.ones_like(right)
        for i in range(planes - 1):
            if step == 0:
                face = f_in[i + side * (planes - 2 - 2 * i)]
                inv = inverse(main + face)
                ratio = face * inv
                factor[i] = ratio
                scale[i] = inv
                main = 1.0 + ratio * main
            else:
                ratio, inv = factor[i], scale[i]
            partial[i] = right * inv
            right = source(i + 1) + ratio * right
        if step == 0:
            edge_out[0] = right
            edge_out[1] = main
            edge_out[2] = f_in[planes - 1]
            first_edge.start()
            first_edge.wait_recv()
            other = edge_got[1]
            face = jnp.where(side == 0, f_in[planes - 1], edge_got[2])
            inv = inverse(main * other + face * (main + other))
            own_weight = (other + face) * inv
            other_weight = face * inv
            value = own_weight * right + other_weight * edge_got[0]
            edge_out[4] = own_weight
            edge_out[5] = other_weight
        else:
            edge_out[3] = right
            second_edge.start()
            second_edge.wait_recv()
            value = edge_out[4] * right + edge_out[5] * edge_got[3]
        for chunk in reversed(range(CHUNKS)):
            for j in reversed(range(chunk * per_chunk, (chunk + 1) * per_chunk)):
                if j == pairs - 1:
                    second = value
                else:
                    second = partial[2 * j + 1] + factor[2 * j + 1] * value
                value = partial[2 * j] + factor[2 * j] * second
                field[2 * j + 1] = second
                field[2 * j] = value
                halo_out[step, 0, j] = both(turned(second[rows - SUB:]), value[rows - SUB:])
                halo_out[step, 1, j] = both(value[:SUB], turned(second[:SUB]))
            start_two(halo_copy(step, chunk, 0), halo_copy(step, chunk, 1))
        if step == 0:
            got_two(*rate_copies)
        for chunk in reversed(range(CHUNKS)):
            got_two(halo_copy(step, chunk, 0), halo_copy(step, chunk, 1))

            def advance_pair(k, carry, chunk=chunk, step=step):
                j = chunk * per_chunk + k
                low, high = halo_got[step, 0, j], halo_got[step, 1, j]
                outer = (both(high, low), turned(both(low, high)))
                for n in range(2):
                    i = 2 * j + n
                    x = plane_of(i)
                    low_rate, high_rate = rate_got[0, i], rate_got[1, i]
                    now = whole(field, i) + [
                        [jnp.where(present, v, 0.0) for v in cut(outer[n])]
                    ]
                    base = whole(rel_in, x) + [cut(both(high_rate, low_rate))]
                    trap = whole(trap_in, x) + [cut(turned(both(low_rate, high_rate)))]
                    for inner in range(SUBSTEPS):
                        now = substep(now, base, trap, inner < SUBSTEPS - 1)
                    for g in range(groups):
                        for b in range(blocks):
                            here = (slice(g * SUB, (g + 1) * SUB), slice(b * LANES, (b + 1) * LANES))
                            if step == STEPS - 1:
                                out[x, here[0], here[1]] = now[g][b]
                            else:
                                field[i, here[0], here[1]] = now[g][b]
                return carry

            lax.fori_loop(0, per_chunk, advance_pair, 0)

    first_edge.wait_send()
    second_edge.wait_send()
    sent_two(*rate_copies)
    for step in range(STEPS):
        for chunk in range(CHUNKS):
            sent_two(halo_copy(step, chunk, 0), halo_copy(step, chunk, 1))


def fused(concentration, face_conductance, release, trap_rate):
    planes, rows, depth = concentration.shape
    block = pltpu.VMEM((planes, rows, depth), jnp.float32)
    return pl.pallas_call(
        kernel,
        out_shape=jax.ShapeDtypeStruct((planes, rows, depth), jnp.float32),
        in_specs=[pl.BlockSpec(memory_space=pl.ANY)] * 4,
        out_specs=pl.BlockSpec(memory_space=pltpu.VMEM),
        scratch_shapes=[block] * 8 + [
            pltpu.VMEM((2, planes, SUB, depth), jnp.float32),
            pltpu.VMEM((2, planes, SUB, depth), jnp.float32),
            pltpu.VMEM((STEPS, 2, planes // 2, SUB, depth), jnp.float32),
            pltpu.VMEM((STEPS, 2, planes // 2, SUB, depth), jnp.float32),
            pltpu.VMEM((6, rows, depth), jnp.float32),
            pltpu.VMEM((6, rows, depth), jnp.float32),
            pltpu.SemaphoreType.DMA((4,)),
            pltpu.SemaphoreType.DMA((2,)),
            pltpu.SemaphoreType.DMA((2,)),
            pltpu.SemaphoreType.DMA((2,)),
            pltpu.SemaphoreType.DMA((2,)),
            pltpu.SemaphoreType.DMA((STEPS, CHUNKS, 2)),
            pltpu.SemaphoreType.DMA((STEPS, CHUNKS, 2)),
        ],
        compiler_params=pltpu.CompilerParams(
            collective_id=0, has_side_effects=True, vmem_limit_bytes=48 * 1024 * 1024
        ),
    )(concentration, face_conductance, release, trap_rate)


def solution(mesh):
    placed = (P("gx", "gy", None), P("gx", "gy", None), P("gx", "gy", None), P("gx", "gy", None))

    def body(concentration, *rest):
        planes, rows, depth = concentration.shape
        fits = (
            mesh.shape["gx"] == 2
            and planes % (2 * CHUNKS) == 0
            and rows % SUB == 0
            and depth % LANES == 0
        )
        return (fused if fits else local)(concentration, *rest)

    return jax.shard_map(
        body, mesh=mesh, in_specs=placed, out_specs=P("gx", "gy", None), check_vma=False
    )
```

```python
import jax
import jax.numpy as jnp
from jax import lax
from jax.experimental import pallas as pl
from jax.experimental.pallas import tpu as pltpu
from jax.sharding import PartitionSpec as P

STEPS = 2
SUBSTEPS = 4


y_weight = 0.32
z_weight = 0.16
time_step = 0.25


def shifted(value, axis, by):
    peers = lax.axis_size(axis)
    pairs = [(i, i + by) for i in range(peers) if 0 <= i + by < peers]
    return lax.ppermute(value, axis, pairs)


def extended_2(block, sides, width):
    for axis, dim in sides:
        count = lax.axis_size(axis)
        forward = [(i, i + 1) for i in range(count - 1)]
        backward = [(target, source) for source, target in forward]
        low = lax.ppermute(
            lax.slice_in_dim(block, block.shape[dim] - width, None, axis=dim), axis, forward
        )
        high = lax.ppermute(lax.slice_in_dim(block, 0, width, axis=dim), axis, backward)
        block = jnp.concatenate([low, block, high], axis=dim)
    return block


def thomas(lower, middle, upper, right):

    def forward(carry, row):
        factor_prev, value_prev = carry
        below_row, main_row, above_row, right_row = row
        divisor = main_row - below_row * factor_prev
        factor = above_row / divisor
        scaled = (right_row - below_row[None] * value_prev) / divisor[None]
        return ((factor, scaled), (factor, scaled))

    start = (jnp.zeros_like(middle[0]), jnp.zeros_like(right[0]))
    unused, (factors, scaled) = lax.scan(forward, start, (lower, middle, upper, right))

    def backward(following, row):
        factor, value = row
        current = value - factor[None] * following
        return (current, current)

    unused, values = lax.scan(backward, jnp.zeros_like(right[0]), (factors, scaled), reverse=True)
    return values


def advance(center, below, above, release, trap_rate):
    left = jnp.concatenate([center[:, :, :1], center[:, :, :-1]], axis=2)
    right = jnp.concatenate([center[:, :, 1:], center[:, :, -1:]], axis=2)
    square = center * center
    reaction = release - trap_rate * square / (1.0 + square)
    return (
        center
        + y_weight * (above + below - 2.0 * center)
        + z_weight * (left + right - 2.0 * center)
        + time_step * reaction
    )


def line_section(field, faces_used):
    rows_x = field.shape[0]
    blank = jnp.zeros_like(faces_used[:1])
    lower = jnp.concatenate([blank, -faces_used[1 : rows_x - 1]], axis=0)
    upper = jnp.concatenate([-faces_used[1 : rows_x - 1], blank], axis=0)
    middle = 1.0 + faces_used[:-1] + faces_used[1:]
    row_index = jnp.arange(rows_x - 1)[:, None, None]
    first_unit = jnp.where(row_index == 0, faces_used[0:1], jnp.float32(0.0))
    last_unit = jnp.where(
        row_index == rows_x - 2, faces_used[rows_x - 1 : rows_x], jnp.float32(0.0)
    )
    right = jnp.stack([field[1:], first_unit, last_unit], axis=1)
    solved = thomas(lower, middle, upper, right)
    inner = solved[:, 0]
    left_part = solved[:, 1]
    right_part = solved[:, 2]
    edge = jnp.stack([faces_used[-1], inner[-1], left_part[-1], right_part[-1]])
    came = shifted(edge, "gx", 1)
    prior_face = came[0]
    own_face = faces_used[0]
    coef_lower = -prior_face * came[2]
    coef_main = 1.0 + prior_face + own_face - prior_face * came[3] - own_face * left_part[0]
    coef_upper = -own_face * right_part[0]
    coef_right = field[0] + prior_face * came[1] + own_face * inner[0]
    system = jnp.stack([coef_lower, coef_main, coef_upper, coef_right])[:, None]
    whole = lax.all_gather(system, "gx", axis=1, tiled=True)
    firsts = thomas(whole[0], whole[1], whole[2], whole[3][:, None])[:, 0]
    position = lax.axis_index("gx")
    count = lax.axis_size("gx")
    first = lax.dynamic_index_in_dim(firsts, position, 0, keepdims=False)
    following = lax.dynamic_index_in_dim(
        firsts, jnp.minimum(position + 1, count - 1), 0, keepdims=False
    )
    rest = inner + first[None] * left_part + following[None] * right_part
    return jnp.concatenate([first[None], rest], axis=0)


def local(concentration, face_conductance, release, trap_rate):
    rows_x = concentration.shape[0]
    rows_y = concentration.shape[1]
    is_last = lax.axis_index("gx") == lax.axis_size("gx") - 1
    inside = jnp.logical_or(
        jnp.arange(rows_x)[:, None, None] < rows_x - 1, jnp.logical_not(is_last)
    )
    faces_used = jnp.where(inside, face_conductance, jnp.float32(0.0))
    field = concentration
    margin = SUBSTEPS
    rates = extended_2(jnp.stack([release, trap_rate]), (("gy", 2),), margin)
    global_rows = lax.axis_index("gy") * rows_y - margin + jnp.arange(rows_y + 2 * margin)
    valid = jnp.logical_and(global_rows >= 0, global_rows < lax.axis_size("gy") * rows_y)
    for step in range(STEPS):
        field = line_section(field, faces_used)
        extended = extended_2(field, (("gy", 1),), margin)
        for substep in range(SUBSTEPS):
            span = extended.shape[1] - 2
            offset = substep + 1
            source_part = rates[0][:, offset : offset + span]
            trap_part = rates[1][:, offset : offset + span]
            keeping = valid[offset : offset + span][None, :, None]
            updated = advance(
                extended[:, 1:-1], extended[:, :-2], extended[:, 2:], source_part, trap_part
            )
            extended = jnp.where(keeping, updated, jnp.float32(0.0))
        field = extended
    return field


SUB = 8
LANES = 128
VMEM_LIMIT = 67_043_328
MESH = pl.DeviceIdType.MESH


def inverse(value):
    return 1.0 / value


def kernel(
    c_hbm, f_hbm, rel_hbm, trap_hbm, out_hbm,
    c_in, f_in, rel_in, trap_in, factor, scale, partial, solved,
    rates, wide, ping, pong, edge_out, edge_got,
    load_sem, store_sem, edge_send, edge_recv, rate_send, rate_recv, halo_send, halo_recv,
):
    blocks, planes, rows, lanes = c_in.shape
    chunks = planes // SUB
    halo = SUBSTEPS
    reach = SUBSTEPS - 1
    side = lax.axis_index("gx")
    spot = lax.axis_index("gy")
    count = lax.axis_size("gy")
    has_prev = spot > 0
    has_next = spot < count - 1
    partner = {"gx": 1 - side}
    to_next = {"gy": jnp.minimum(spot + 1, count - 1)}
    to_prev = {"gy": jnp.maximum(spot - 1, 0)}
    every = range(blocks)

    loads = []
    for n, (src, dst) in enumerate(
        ((rel_hbm, rel_in), (trap_hbm, trap_in), (f_hbm, f_in), (c_hbm, c_in))
    ):
        loads.append([
            pltpu.make_async_copy(
                src.at[:, :, pl.ds(b * lanes, lanes)], dst.at[b], load_sem.at[n, b]
            )
            for b in every
        ])
    for load in loads:
        for part in load:
            part.start()

    barrier = pltpu.get_barrier_semaphore()
    pl.semaphore_signal(barrier, inc=1, device_id=partner, device_id_type=MESH)

    @pl.when(has_next)
    def _():
        pl.semaphore_signal(barrier, inc=1, device_id=to_next, device_id_type=MESH)

    @pl.when(has_prev)
    def _():
        pl.semaphore_signal(barrier, inc=1, device_id=to_prev, device_id_type=MESH)

    def remote(src, dst, send, recv, target):
        return pltpu.make_async_remote_copy(
            src_ref=src, dst_ref=dst, send_sem=send, recv_sem=recv,
            device_id=target, device_id_type=MESH,
        )

    rate_copies = (
        remote(
            rates.at[:, pl.ds(rows, reach)], rates.at[:, pl.ds(0, reach)],
            rate_send.at[0], rate_recv.at[0], to_next,
        ),
        remote(
            rates.at[:, pl.ds(reach, reach)], rates.at[:, pl.ds(rows + reach, reach)],
            rate_send.at[1], rate_recv.at[1], to_prev,
        ),
    )

    def chunk_of(k):
        return chunks - 1 - k + side * (2 * k - chunks + 1)

    def halo_copies(step, k):
        part = wide.at[step, chunk_of(k)]
        return (
            remote(
                part.at[pl.ds(rows, halo)], part.at[pl.ds(0, halo)],
                halo_send.at[step, k, 0], halo_recv.at[step, k, 0], to_next,
            ),
            remote(
                part.at[pl.ds(halo, halo)], part.at[pl.ds(rows + halo, halo)],
                halo_send.at[step, k, 1], halo_recv.at[step, k, 1], to_prev,
            ),
        )

    def start_two(first, second):
        @pl.when(has_next)
        def _():
            first.start()

        @pl.when(has_prev)
        def _():
            second.start()

    def got_two(first, second):
        @pl.when(has_prev)
        def _():
            first.wait_recv()

        @pl.when(has_next)
        def _():
            second.wait_recv()

    def sent_two(first, second):
        @pl.when(has_next)
        def _():
            first.wait_send()

        @pl.when(has_prev)
        def _():
            second.wait_send()

    def flat(ref, b):
        return ref.at[b].reshape(planes * rows, lanes)

    def across(group, y):
        return pl.ds(group * (SUB * rows) + y, SUB, stride=rows)

    for load in loads[:2]:
        for part in load:
            part.wait()

    def prepare(group, carry):
        for y in range(rows):
            for b in every:
                trap = time_step * flat(trap_in, b)[across(group, y), :]
                release = time_step * flat(rel_in, b)[across(group, y), :]
                rates[0, reach + y, group, b] = release - trap
                rates[1, reach + y, group, b] = trap
        return carry

    lax.fori_loop(0, chunks, prepare, 0)

    pl.semaphore_wait(barrier, 1 + has_prev.astype(jnp.int32) + has_next.astype(jnp.int32))
    start_two(*rate_copies)

    for load in loads[2:]:
        for part in load:
            part.wait()

    edge_copies = (
        remote(
            edge_out.at[pl.ds(0, 3)], edge_got.at[pl.ds(0, 3)],
            edge_send.at[0], edge_recv.at[0], partner,
        ),
        remote(edge_out.at[3], edge_got.at[3], edge_send.at[1], edge_recv.at[1], partner),
    )

    lane = lax.broadcasted_iota(jnp.int32, (SUB, lanes), 1)
    lane_first, lane_last = lane == 0, lane == lanes - 1

    def substep(inner, read, group, write):
        span = rows + 2 * (reach - inner)
        start = -(reach - inner)

        def clean(y, value):
            if y < 0:
                return jnp.where(has_prev, value, 0.0)
            if y >= rows:
                return jnp.where(has_next, value, 0.0)
            return value

        def fetch(y):
            got = [read(y, b) for b in every]
            return [clean(y, v) for v in got] if inner == 0 else got

        window = [fetch(start - 1), fetch(start)]
        for y in range(start, start + span):
            window.append(fetch(y + 1))
            above, center, below = window[-3:]
            window = window[-2:]
            right = [pltpu.roll(v, 1, axis=1) for v in center]
            left = [pltpu.roll(v, lanes - 1, axis=1) for v in center]
            for b in every:
                c = center[b]
                lower = jnp.where(lane_first, right[b - 1] if b > 0 else c, right[b])
                upper = jnp.where(lane_last, left[b + 1] if b < blocks - 1 else c, left[b])
                value = (
                    (1.0 - 2.0 * y_weight - 2.0 * z_weight) * c
                    + y_weight * (above[b] + below[b])
                    + z_weight * (lower + upper)
                    + (
                        rates[0, reach + y, group, b]
                        + rates[1, reach + y, group, b] * inverse(1.0 + c * c)
                    )
                )
                write(y, b, clean(y, value))

    def plane(ref, x):
        return [ref[b, x] for b in every]

    for step in range(STEPS):
        def position(i):
            return i + side * (planes - 1 - 2 * i)

        right = plane(c_in, position(0))
        if step == 0:
            main = [jnp.ones_like(v) for v in right]
        for i in range(planes - 1):
            if step == 0:
                face = plane(f_in, i + side * (planes - 2 - 2 * i))
                inv = [inverse(main[b] + face[b]) for b in every]
                ratio = [face[b] * inv[b] for b in every]
                for b in every:
                    factor[i, b] = ratio[b]
                    scale[i, b] = inv[b]
                main = [1.0 + ratio[b] * main[b] for b in every]
            else:
                ratio = [factor[i, b] for b in every]
                inv = [scale[i, b] for b in every]
            following = plane(c_in, position(i + 1))
            for b in every:
                partial[i, b] = right[b] * inv[b]
            right = [following[b] + ratio[b] * right[b] for b in every]
        if step == 0:
            for b in every:
                edge_out[0, b] = right[b]
                edge_out[1, b] = main[b]
                edge_out[2, b] = f_in[b, planes - 1]
            edge_copies[0].start()
            edge_copies[0].wait_recv()
            value = []
            for b in every:
                other = edge_got[1, b]
                face = jnp.where(side == 0, f_in[b, planes - 1], edge_got[2, b])
                inv = inverse(main[b] * other + face * (main[b] + other))
                own_weight = (other + face) * inv
                other_weight = face * inv
                value.append(own_weight * right[b] + other_weight * edge_got[0, b])
                edge_out[4, b] = own_weight
                edge_out[5, b] = other_weight
        else:
            for b in every:
                edge_out[3, b] = right[b]
            edge_copies[1].start()
            edge_copies[1].wait_recv()
            value = [
                edge_out[4, b] * right[b] + edge_out[5, b] * edge_got[3, b] for b in every
            ]
        for k in range(chunks):
            for i in reversed(range((chunks - 1 - k) * SUB, (chunks - k) * SUB)):
                if i < planes - 1:
                    value = [partial[i, b] + factor[i, b] * value[b] for b in every]
                for b in every:
                    solved[b, position(i)] = value[b]
            group = chunk_of(k)
            for y in range(rows):
                for b in every:
                    wide[step, group, halo + y, b] = flat(solved, b)[across(group, y), :]
            start_two(*halo_copies(step, k))
        if step == 0:
            got_two(*rate_copies)

        def finish(k, carry, step=step):
            group = chunk_of(k)
            got_two(*halo_copies(step, k))

            def first(y, b):
                return wide[step, group, halo + y, b]

            def reader(ref):
                return lambda y, b: ref[halo + y, b]

            def writer(ref):
                def put(y, b, value):
                    ref[halo + y, b] = value
                return put

            def last(y, b, value):
                flat(c_in, b)[across(group, y), :] = value

            read = first
            for inner in range(SUBSTEPS):
                target = (ping, pong)[inner % 2]
                write = last if inner == SUBSTEPS - 1 else writer(target)
                substep(inner, read, group, write)
                read = reader(target)
            if step == STEPS - 1:
                for b in every:
                    store(group, b).start()
            return carry

        def store(group, b):
            part = pl.ds(group * SUB, SUB)
            return pltpu.make_async_copy(
                c_in.at[b, part],
                out_hbm.at[part, :, pl.ds(b * lanes, lanes)],
                store_sem.at[group, b],
            )

        lax.fori_loop(0, chunks, finish, 0)

    for copy in edge_copies:
        copy.wait_send()
    sent_two(*rate_copies)
    for step in range(STEPS):
        for k in range(chunks):
            sent_two(*halo_copies(step, k))
    for group in range(chunks):
        for b in every:
            store(group, b).wait()


def fused(concentration, face_conductance, release, trap_rate):
    planes, rows, depth = concentration.shape
    blocks, chunks = depth // LANES, planes // SUB
    block = pltpu.VMEM((blocks, planes, rows, LANES), jnp.float32)
    kept = pltpu.VMEM((planes, blocks, rows, LANES), jnp.float32)
    edge = pltpu.VMEM((6, blocks, rows, LANES), jnp.float32)
    stage = pltpu.VMEM((rows + 2 * SUBSTEPS, blocks, SUB, LANES), jnp.float32)
    return pl.pallas_call(
        kernel,
        out_shape=jax.ShapeDtypeStruct((planes, rows, depth), jnp.float32),
        in_specs=[pl.BlockSpec(memory_space=pl.ANY)] * 4,
        out_specs=pl.BlockSpec(memory_space=pl.ANY),
        scratch_shapes=[block] * 4 + [kept] * 3 + [block] + [
            pltpu.VMEM(
                (2, rows + 2 * (SUBSTEPS - 1), chunks, blocks, SUB, LANES), jnp.float32
            ),
            pltpu.VMEM(
                (STEPS, chunks, rows + 2 * SUBSTEPS, blocks, SUB, LANES), jnp.float32
            ),
            stage, stage, edge, edge,
            pltpu.SemaphoreType.DMA((4, blocks)),
            pltpu.SemaphoreType.DMA((chunks, blocks)),
            pltpu.SemaphoreType.DMA((2,)),
            pltpu.SemaphoreType.DMA((2,)),
            pltpu.SemaphoreType.DMA((2,)),
            pltpu.SemaphoreType.DMA((2,)),
            pltpu.SemaphoreType.DMA((STEPS, chunks, 2)),
            pltpu.SemaphoreType.DMA((STEPS, chunks, 2)),
        ],
        compiler_params=pltpu.CompilerParams(
            collective_id=0, has_side_effects=True, vmem_limit_bytes=VMEM_LIMIT
        ),
    )(concentration, face_conductance, release, trap_rate)


def solution(mesh):
    placed = (P("gx", "gy", None), P("gx", "gy", None), P("gx", "gy", None), P("gx", "gy", None))

    def body(concentration, *rest):
        planes, rows, depth = concentration.shape
        fits = (
            mesh.shape["gx"] == 2
            and planes % SUB == 0
            and rows >= 2 * SUBSTEPS
            and rows % SUB == 0
            and depth % LANES == 0
        )
        return (fused if fits else local)(concentration, *rest)

    return jax.shard_map(
        body, mesh=mesh, in_specs=placed, out_specs=P("gx", "gy", None), check_vma=False
    )
```

```python
import jax
import jax.numpy as jnp
from jax import lax
from jax.experimental import pallas as pl
from jax.experimental.pallas import tpu as pltpu
from jax.sharding import PartitionSpec as P

STEPS = 2
SUBSTEPS = 4


y_weight = 0.32
z_weight = 0.16
time_step = 0.25


def shifted(value, axis, by):
    peers = lax.axis_size(axis)
    pairs = [(i, i + by) for i in range(peers) if 0 <= i + by < peers]
    return lax.ppermute(value, axis, pairs)


def extended_2(block, sides, width):
    for axis, dim in sides:
        count = lax.axis_size(axis)
        forward = [(i, i + 1) for i in range(count - 1)]
        backward = [(target, source) for source, target in forward]
        low = lax.ppermute(
            lax.slice_in_dim(block, block.shape[dim] - width, None, axis=dim), axis, forward
        )
        high = lax.ppermute(lax.slice_in_dim(block, 0, width, axis=dim), axis, backward)
        block = jnp.concatenate([low, block, high], axis=dim)
    return block


def thomas(lower, middle, upper, right):

    def forward(carry, row):
        factor_prev, value_prev = carry
        below_row, main_row, above_row, right_row = row
        divisor = main_row - below_row * factor_prev
        factor = above_row / divisor
        scaled = (right_row - below_row[None] * value_prev) / divisor[None]
        return ((factor, scaled), (factor, scaled))

    start = (jnp.zeros_like(middle[0]), jnp.zeros_like(right[0]))
    unused, (factors, scaled) = lax.scan(forward, start, (lower, middle, upper, right))

    def backward(following, row):
        factor, value = row
        current = value - factor[None] * following
        return (current, current)

    unused, values = lax.scan(backward, jnp.zeros_like(right[0]), (factors, scaled), reverse=True)
    return values


def advance(center, below, above, release, trap_rate):
    left = jnp.concatenate([center[:, :, :1], center[:, :, :-1]], axis=2)
    right = jnp.concatenate([center[:, :, 1:], center[:, :, -1:]], axis=2)
    square = center * center
    reaction = release - trap_rate * square / (1.0 + square)
    return (
        center
        + y_weight * (above + below - 2.0 * center)
        + z_weight * (left + right - 2.0 * center)
        + time_step * reaction
    )


def line_section(field, faces_used):
    rows_x = field.shape[0]
    blank = jnp.zeros_like(faces_used[:1])
    lower = jnp.concatenate([blank, -faces_used[1 : rows_x - 1]], axis=0)
    upper = jnp.concatenate([-faces_used[1 : rows_x - 1], blank], axis=0)
    middle = 1.0 + faces_used[:-1] + faces_used[1:]
    row_index = jnp.arange(rows_x - 1)[:, None, None]
    first_unit = jnp.where(row_index == 0, faces_used[0:1], jnp.float32(0.0))
    last_unit = jnp.where(
        row_index == rows_x - 2, faces_used[rows_x - 1 : rows_x], jnp.float32(0.0)
    )
    right = jnp.stack([field[1:], first_unit, last_unit], axis=1)
    solved = thomas(lower, middle, upper, right)
    inner = solved[:, 0]
    left_part = solved[:, 1]
    right_part = solved[:, 2]
    edge = jnp.stack([faces_used[-1], inner[-1], left_part[-1], right_part[-1]])
    came = shifted(edge, "gx", 1)
    prior_face = came[0]
    own_face = faces_used[0]
    coef_lower = -prior_face * came[2]
    coef_main = 1.0 + prior_face + own_face - prior_face * came[3] - own_face * left_part[0]
    coef_upper = -own_face * right_part[0]
    coef_right = field[0] + prior_face * came[1] + own_face * inner[0]
    system = jnp.stack([coef_lower, coef_main, coef_upper, coef_right])[:, None]
    whole = lax.all_gather(system, "gx", axis=1, tiled=True)
    firsts = thomas(whole[0], whole[1], whole[2], whole[3][:, None])[:, 0]
    position = lax.axis_index("gx")
    count = lax.axis_size("gx")
    first = lax.dynamic_index_in_dim(firsts, position, 0, keepdims=False)
    following = lax.dynamic_index_in_dim(
        firsts, jnp.minimum(position + 1, count - 1), 0, keepdims=False
    )
    rest = inner + first[None] * left_part + following[None] * right_part
    return jnp.concatenate([first[None], rest], axis=0)


def local(concentration, face_conductance, release, trap_rate):
    rows_x = concentration.shape[0]
    rows_y = concentration.shape[1]
    is_last = lax.axis_index("gx") == lax.axis_size("gx") - 1
    inside = jnp.logical_or(
        jnp.arange(rows_x)[:, None, None] < rows_x - 1, jnp.logical_not(is_last)
    )
    faces_used = jnp.where(inside, face_conductance, jnp.float32(0.0))
    field = concentration
    margin = SUBSTEPS
    rates = extended_2(jnp.stack([release, trap_rate]), (("gy", 2),), margin)
    global_rows = lax.axis_index("gy") * rows_y - margin + jnp.arange(rows_y + 2 * margin)
    valid = jnp.logical_and(global_rows >= 0, global_rows < lax.axis_size("gy") * rows_y)
    for step in range(STEPS):
        field = line_section(field, faces_used)
        extended = extended_2(field, (("gy", 1),), margin)
        for substep in range(SUBSTEPS):
            span = extended.shape[1] - 2
            offset = substep + 1
            source_part = rates[0][:, offset : offset + span]
            trap_part = rates[1][:, offset : offset + span]
            keeping = valid[offset : offset + span][None, :, None]
            updated = advance(
                extended[:, 1:-1], extended[:, :-2], extended[:, 2:], source_part, trap_part
            )
            extended = jnp.where(keeping, updated, jnp.float32(0.0))
        field = extended
    return field


SUB = 8
LANES = 128
VMEM_LIMIT = 67_043_328
MESH = pl.DeviceIdType.MESH


def inverse(value):
    return 1.0 / value


def kernel(
    c_hbm, f_hbm, rel_hbm, trap_hbm, out_hbm,
    c_in, f_in, rel_in, trap_in, factor, scale, partial, solved,
    rates, wide, levels, edge_out, edge_got,
    load_sem, store_sem, edge_send, edge_recv, rate_send, rate_recv, halo_send, halo_recv,
):
    blocks, planes, rows, lanes = c_in.shape
    chunks = planes // SUB
    halo = SUBSTEPS
    reach = SUBSTEPS - 1
    side = lax.axis_index("gx")
    spot = lax.axis_index("gy")
    count = lax.axis_size("gy")
    has_prev = spot > 0
    has_next = spot < count - 1
    partner = {"gx": 1 - side}
    to_next = {"gy": jnp.minimum(spot + 1, count - 1)}
    to_prev = {"gy": jnp.maximum(spot - 1, 0)}
    every = range(blocks)

    loads = []
    for n, (src, dst) in enumerate(
        ((rel_hbm, rel_in), (trap_hbm, trap_in), (f_hbm, f_in), (c_hbm, c_in))
    ):
        loads.append([
            pltpu.make_async_copy(
                src.at[:, :, pl.ds(b * lanes, lanes)], dst.at[b], load_sem.at[n, b]
            )
            for b in every
        ])
    for load in loads:
        for part in load:
            part.start()

    barrier = pltpu.get_barrier_semaphore()
    pl.semaphore_signal(barrier, inc=1, device_id=partner, device_id_type=MESH)

    @pl.when(has_next)
    def _():
        pl.semaphore_signal(barrier, inc=1, device_id=to_next, device_id_type=MESH)

    @pl.when(has_prev)
    def _():
        pl.semaphore_signal(barrier, inc=1, device_id=to_prev, device_id_type=MESH)

    def remote(src, dst, send, recv, target):
        return pltpu.make_async_remote_copy(
            src_ref=src, dst_ref=dst, send_sem=send, recv_sem=recv,
            device_id=target, device_id_type=MESH,
        )

    rate_copies = (
        remote(
            rates.at[:, pl.ds(rows, reach)], rates.at[:, pl.ds(0, reach)],
            rate_send.at[0], rate_recv.at[0], to_next,
        ),
        remote(
            rates.at[:, pl.ds(reach, reach)], rates.at[:, pl.ds(rows + reach, reach)],
            rate_send.at[1], rate_recv.at[1], to_prev,
        ),
    )

    def chunk_of(k):
        return chunks - 1 - k + side * (2 * k - chunks + 1)

    def halo_copies(step, k):
        part = wide.at[step, chunk_of(k)]
        return (
            remote(
                part.at[pl.ds(rows, halo)], part.at[pl.ds(0, halo)],
                halo_send.at[step, k, 0], halo_recv.at[step, k, 0], to_next,
            ),
            remote(
                part.at[pl.ds(halo, halo)], part.at[pl.ds(rows + halo, halo)],
                halo_send.at[step, k, 1], halo_recv.at[step, k, 1], to_prev,
            ),
        )

    def start_two(first, second):
        @pl.when(has_next)
        def _():
            first.start()

        @pl.when(has_prev)
        def _():
            second.start()

    def got_two(first, second):
        @pl.when(has_prev)
        def _():
            first.wait_recv()

        @pl.when(has_next)
        def _():
            second.wait_recv()

    def sent_two(first, second):
        @pl.when(has_next)
        def _():
            first.wait_send()

        @pl.when(has_prev)
        def _():
            second.wait_send()

    def flat(ref, b):
        return ref.at[b].reshape(planes * rows, lanes)

    def across(group, y):
        return pl.ds(group * (SUB * rows) + y, SUB, stride=rows)

    for load in loads[:2]:
        for part in load:
            part.wait()

    def prepare(spans):
        def body(group, carry):
            for y in [y for span in spans for y in span]:
                for b in every:
                    trap = time_step * flat(trap_in, b)[across(group, y), :]
                    release = time_step * flat(rel_in, b)[across(group, y), :]
                    rates[0, reach + y, group, b] = release - trap
                    rates[1, reach + y, group, b] = trap
            return carry

        lax.fori_loop(0, chunks, body, 0)

    prepare((range(reach), range(rows - reach, rows)))

    pl.semaphore_wait(barrier, 1 + has_prev.astype(jnp.int32) + has_next.astype(jnp.int32))
    start_two(*rate_copies)

    for load in loads[2:]:
        for part in load:
            part.wait()

    edge_copies = (
        remote(
            edge_out.at[pl.ds(0, 3)], edge_got.at[pl.ds(0, 3)],
            edge_send.at[0], edge_recv.at[0], partner,
        ),
        remote(edge_out.at[3], edge_got.at[3], edge_send.at[1], edge_recv.at[1], partner),
    )

    lane = lax.broadcasted_iota(jnp.int32, (SUB, lanes), 1)
    lane_first, lane_last = lane == 0, lane == lanes - 1

    def substep(inner, span, read, group, write):
        start = span[0]

        def clean(y, value):
            if y < 0:
                return jnp.where(has_prev, value, 0.0)
            if y >= rows:
                return jnp.where(has_next, value, 0.0)
            return value

        def fetch(y):
            got = [read(y, b) for b in every]
            return [clean(y, v) for v in got] if inner == 0 else got

        window = [fetch(start - 1), fetch(start)]
        for y in span:
            window.append(fetch(y + 1))
            above, center, below = window[-3:]
            window = window[-2:]
            right = [pltpu.roll(v, 1, axis=1) for v in center]
            left = [pltpu.roll(v, lanes - 1, axis=1) for v in center]
            for b in every:
                c = center[b]
                lower = jnp.where(lane_first, right[b - 1] if b > 0 else c, right[b])
                upper = jnp.where(lane_last, left[b + 1] if b < blocks - 1 else c, left[b])
                value = (
                    (1.0 - 2.0 * y_weight - 2.0 * z_weight) * c
                    + y_weight * (above[b] + below[b])
                    + z_weight * (lower + upper)
                    + (
                        rates[0, reach + y, group, b]
                        + rates[1, reach + y, group, b] * inverse(1.0 + c * c)
                    )
                )
                write(y, b, clean(y, value))

    def plane(ref, x):
        return [ref[b, x] for b in every]

    for step in range(STEPS):
        def position(i):
            return i + side * (planes - 1 - 2 * i)

        right = plane(c_in, position(0))
        if step == 0:
            main = [jnp.ones_like(v) for v in right]
        for i in range(planes - 1):
            if step == 0:
                face = plane(f_in, i + side * (planes - 2 - 2 * i))
                inv = [inverse(main[b] + face[b]) for b in every]
                ratio = [face[b] * inv[b] for b in every]
                for b in every:
                    factor[i, b] = ratio[b]
                    scale[i, b] = inv[b]
                main = [1.0 + ratio[b] * main[b] for b in every]
            else:
                ratio = [factor[i, b] for b in every]
                inv = [scale[i, b] for b in every]
            following = plane(c_in, position(i + 1))
            for b in every:
                partial[i, b] = right[b] * inv[b]
            right = [following[b] + ratio[b] * right[b] for b in every]
        if step == 0:
            for b in every:
                edge_out[0, b] = right[b]
                edge_out[1, b] = main[b]
                edge_out[2, b] = f_in[b, planes - 1]
            edge_copies[0].start()
            prepare((range(reach, rows - reach),))
            edge_copies[0].wait_recv()
            value = []
            for b in every:
                other = edge_got[1, b]
                face = jnp.where(side == 0, f_in[b, planes - 1], edge_got[2, b])
                inv = inverse(main[b] * other + face * (main[b] + other))
                own_weight = (other + face) * inv
                other_weight = face * inv
                value.append(own_weight * right[b] + other_weight * edge_got[0, b])
                edge_out[4, b] = own_weight
                edge_out[5, b] = other_weight
        else:
            for b in every:
                edge_out[3, b] = right[b]
            edge_copies[1].start()
            edge_copies[1].wait_recv()
            value = [
                edge_out[4, b] * right[b] + edge_out[5, b] * edge_got[3, b] for b in every
            ]
        for k in range(chunks):
            for i in reversed(range((chunks - 1 - k) * SUB, (chunks - k) * SUB)):
                if i < planes - 1:
                    value = [partial[i, b] + factor[i, b] * value[b] for b in every]
                for b in every:
                    solved[b, position(i)] = value[b]
            group = chunk_of(k)
            for y in range(rows):
                for b in every:
                    wide[step, group, halo + y, b] = flat(solved, b)[across(group, y), :]
            start_two(*halo_copies(step, k))

        def run(group, spans_of, step=step):
            def first(y, b):
                return wide[step, group, halo + y, b]

            def level(inner):
                return lambda y, b: levels[inner, group, halo + y, b]

            def keep(inner):
                def put(y, b, value):
                    levels[inner, group, halo + y, b] = value
                return put

            def last(y, b, value):
                flat(c_in, b)[across(group, y), :] = value

            for inner in range(SUBSTEPS):
                for span in spans_of(inner):
                    substep(
                        inner, span,
                        first if inner == 0 else level(inner - 1),
                        group,
                        last if inner == SUBSTEPS - 1 else keep(inner),
                    )

        def inside(k, carry):
            run(chunk_of(k), lambda inner: (range(inner + 1, rows - 1 - inner),))
            return carry

        def finish(k, carry, step=step):
            group = chunk_of(k)
            got_two(*halo_copies(step, k))
            run(group, lambda inner: (
                range(inner - reach, inner + 1),
                range(rows - 1 - inner, rows + reach - inner),
            ))
            if step == STEPS - 1:
                for b in every:
                    store(group, b).start()
            return carry

        def store(group, b):
            part = pl.ds(group * SUB, SUB)
            return pltpu.make_async_copy(
                c_in.at[b, part],
                out_hbm.at[part, :, pl.ds(b * lanes, lanes)],
                store_sem.at[group, b],
            )

        lax.fori_loop(0, chunks, inside, 0)
        if step == 0:
            got_two(*rate_copies)
        lax.fori_loop(0, chunks, finish, 0)

    for copy in edge_copies:
        copy.wait_send()
    sent_two(*rate_copies)
    for step in range(STEPS):
        for k in range(chunks):
            sent_two(*halo_copies(step, k))
    for group in range(chunks):
        for b in every:
            store(group, b).wait()


def fused(concentration, face_conductance, release, trap_rate):
    planes, rows, depth = concentration.shape
    blocks, chunks = depth // LANES, planes // SUB
    block = pltpu.VMEM((blocks, planes, rows, LANES), jnp.float32)
    kept = pltpu.VMEM((planes, blocks, rows, LANES), jnp.float32)
    edge = pltpu.VMEM((6, blocks, rows, LANES), jnp.float32)
    stage = pltpu.VMEM(
        (SUBSTEPS - 1, chunks, rows + 2 * SUBSTEPS, blocks, SUB, LANES), jnp.float32
    )
    parts = pl.pallas_call(
        kernel,
        out_shape=jax.ShapeDtypeStruct((planes, rows, depth), jnp.float32),
        in_specs=[pl.BlockSpec(memory_space=pl.ANY)] * 4,
        out_specs=pl.BlockSpec(memory_space=pl.ANY),
        scratch_shapes=[block] * 4 + [kept] * 3 + [block] + [
            pltpu.VMEM(
                (2, rows + 2 * (SUBSTEPS - 1), chunks, blocks, SUB, LANES), jnp.float32
            ),
            pltpu.VMEM(
                (STEPS, chunks, rows + 2 * SUBSTEPS, blocks, SUB, LANES), jnp.float32
            ),
            stage, edge, edge,
            pltpu.SemaphoreType.DMA((4, blocks)),
            pltpu.SemaphoreType.DMA((chunks, blocks)),
            pltpu.SemaphoreType.DMA((2,)),
            pltpu.SemaphoreType.DMA((2,)),
            pltpu.SemaphoreType.DMA((2,)),
            pltpu.SemaphoreType.DMA((2,)),
            pltpu.SemaphoreType.DMA((STEPS, chunks, 2)),
            pltpu.SemaphoreType.DMA((STEPS, chunks, 2)),
        ],
        compiler_params=pltpu.CompilerParams(
            collective_id=0, has_side_effects=True, vmem_limit_bytes=VMEM_LIMIT
        ),
    )(concentration, face_conductance, release, trap_rate)
    return parts


def solution(mesh):
    placed = (P("gx", "gy", None), P("gx", "gy", None), P("gx", "gy", None), P("gx", "gy", None))

    def body(concentration, *rest):
        planes, rows, depth = concentration.shape
        fits = (
            mesh.shape["gx"] == 2
            and planes % SUB == 0
            and rows >= 2 * SUBSTEPS
            and rows % SUB == 0
            and depth % LANES == 0
        )
        return (fused if fits else local)(concentration, *rest)

    return jax.shard_map(
        body, mesh=mesh, in_specs=placed, out_specs=P("gx", "gy", None), check_vma=False
    )
```

```python
import jax
import jax.numpy as jnp
from jax import lax
from jax.experimental import pallas as pl
from jax.experimental.pallas import tpu as pltpu
from jax.sharding import PartitionSpec as P

STEPS = 2
SUBSTEPS = 4


y_weight = 0.32
z_weight = 0.16
time_step = 0.25


def shifted(value, axis, by):
    peers = lax.axis_size(axis)
    pairs = [(i, i + by) for i in range(peers) if 0 <= i + by < peers]
    return lax.ppermute(value, axis, pairs)


def extended_2(block, sides, width):
    for axis, dim in sides:
        count = lax.axis_size(axis)
        forward = [(i, i + 1) for i in range(count - 1)]
        backward = [(target, source) for source, target in forward]
        low = lax.ppermute(
            lax.slice_in_dim(block, block.shape[dim] - width, None, axis=dim), axis, forward
        )
        high = lax.ppermute(lax.slice_in_dim(block, 0, width, axis=dim), axis, backward)
        block = jnp.concatenate([low, block, high], axis=dim)
    return block


def thomas(lower, middle, upper, right):

    def forward(carry, row):
        factor_prev, value_prev = carry
        below_row, main_row, above_row, right_row = row
        divisor = main_row - below_row * factor_prev
        factor = above_row / divisor
        scaled = (right_row - below_row[None] * value_prev) / divisor[None]
        return ((factor, scaled), (factor, scaled))

    start = (jnp.zeros_like(middle[0]), jnp.zeros_like(right[0]))
    unused, (factors, scaled) = lax.scan(forward, start, (lower, middle, upper, right))

    def backward(following, row):
        factor, value = row
        current = value - factor[None] * following
        return (current, current)

    unused, values = lax.scan(backward, jnp.zeros_like(right[0]), (factors, scaled), reverse=True)
    return values


def advance(center, below, above, release, trap_rate):
    left = jnp.concatenate([center[:, :, :1], center[:, :, :-1]], axis=2)
    right = jnp.concatenate([center[:, :, 1:], center[:, :, -1:]], axis=2)
    square = center * center
    reaction = release - trap_rate * square / (1.0 + square)
    return (
        center
        + y_weight * (above + below - 2.0 * center)
        + z_weight * (left + right - 2.0 * center)
        + time_step * reaction
    )


def line_section(field, faces_used):
    rows_x = field.shape[0]
    blank = jnp.zeros_like(faces_used[:1])
    lower = jnp.concatenate([blank, -faces_used[1 : rows_x - 1]], axis=0)
    upper = jnp.concatenate([-faces_used[1 : rows_x - 1], blank], axis=0)
    middle = 1.0 + faces_used[:-1] + faces_used[1:]
    row_index = jnp.arange(rows_x - 1)[:, None, None]
    first_unit = jnp.where(row_index == 0, faces_used[0:1], jnp.float32(0.0))
    last_unit = jnp.where(
        row_index == rows_x - 2, faces_used[rows_x - 1 : rows_x], jnp.float32(0.0)
    )
    right = jnp.stack([field[1:], first_unit, last_unit], axis=1)
    solved = thomas(lower, middle, upper, right)
    inner = solved[:, 0]
    left_part = solved[:, 1]
    right_part = solved[:, 2]
    edge = jnp.stack([faces_used[-1], inner[-1], left_part[-1], right_part[-1]])
    came = shifted(edge, "gx", 1)
    prior_face = came[0]
    own_face = faces_used[0]
    coef_lower = -prior_face * came[2]
    coef_main = 1.0 + prior_face + own_face - prior_face * came[3] - own_face * left_part[0]
    coef_upper = -own_face * right_part[0]
    coef_right = field[0] + prior_face * came[1] + own_face * inner[0]
    system = jnp.stack([coef_lower, coef_main, coef_upper, coef_right])[:, None]
    whole = lax.all_gather(system, "gx", axis=1, tiled=True)
    firsts = thomas(whole[0], whole[1], whole[2], whole[3][:, None])[:, 0]
    position = lax.axis_index("gx")
    count = lax.axis_size("gx")
    first = lax.dynamic_index_in_dim(firsts, position, 0, keepdims=False)
    following = lax.dynamic_index_in_dim(
        firsts, jnp.minimum(position + 1, count - 1), 0, keepdims=False
    )
    rest = inner + first[None] * left_part + following[None] * right_part
    return jnp.concatenate([first[None], rest], axis=0)


def local(concentration, face_conductance, release, trap_rate):
    rows_x = concentration.shape[0]
    rows_y = concentration.shape[1]
    is_last = lax.axis_index("gx") == lax.axis_size("gx") - 1
    inside = jnp.logical_or(
        jnp.arange(rows_x)[:, None, None] < rows_x - 1, jnp.logical_not(is_last)
    )
    faces_used = jnp.where(inside, face_conductance, jnp.float32(0.0))
    field = concentration
    margin = SUBSTEPS
    rates = extended_2(jnp.stack([release, trap_rate]), (("gy", 2),), margin)
    global_rows = lax.axis_index("gy") * rows_y - margin + jnp.arange(rows_y + 2 * margin)
    valid = jnp.logical_and(global_rows >= 0, global_rows < lax.axis_size("gy") * rows_y)
    for step in range(STEPS):
        field = line_section(field, faces_used)
        extended = extended_2(field, (("gy", 1),), margin)
        for substep in range(SUBSTEPS):
            span = extended.shape[1] - 2
            offset = substep + 1
            source_part = rates[0][:, offset : offset + span]
            trap_part = rates[1][:, offset : offset + span]
            keeping = valid[offset : offset + span][None, :, None]
            updated = advance(
                extended[:, 1:-1], extended[:, :-2], extended[:, 2:], source_part, trap_part
            )
            extended = jnp.where(keeping, updated, jnp.float32(0.0))
        field = extended
    return field


SUB = 8
LANES = 128
VMEM_LIMIT = 67_043_328 - 1200 * 1024
MESH = pl.DeviceIdType.MESH


def inverse(value):
    return 1.0 / value


def kernel(
    c_hbm, f_hbm, rel_hbm, trap_hbm, out,
    c_in, f_in, rel_in, trap_in, factor, scale, partial, solved,
    rates, wide, levels, edge_out, edge_got,
    load_sem, edge_send, edge_recv, rate_send, rate_recv, halo_send, halo_recv,
):
    blocks, planes, rows, lanes = c_in.shape
    chunks = planes // SUB
    halo = SUBSTEPS
    reach = SUBSTEPS - 1
    side = lax.axis_index("gx")
    spot = lax.axis_index("gy")
    count = lax.axis_size("gy")
    has_prev = spot > 0
    has_next = spot < count - 1
    partner = {"gx": 1 - side}
    to_next = {"gy": jnp.minimum(spot + 1, count - 1)}
    to_prev = {"gy": jnp.maximum(spot - 1, 0)}
    every = range(blocks)

    loads = []
    for n, (src, dst) in enumerate(
        ((rel_hbm, rel_in), (trap_hbm, trap_in), (f_hbm, f_in), (c_hbm, c_in))
    ):
        loads.append([
            pltpu.make_async_copy(
                src.at[:, :, pl.ds(b * lanes, lanes)], dst.at[b], load_sem.at[n, b]
            )
            for b in every
        ])
    for load in loads:
        for part in load:
            part.start()

    barrier = pltpu.get_barrier_semaphore()
    pl.semaphore_signal(barrier, inc=1, device_id=partner, device_id_type=MESH)

    @pl.when(has_next)
    def _():
        pl.semaphore_signal(barrier, inc=1, device_id=to_next, device_id_type=MESH)

    @pl.when(has_prev)
    def _():
        pl.semaphore_signal(barrier, inc=1, device_id=to_prev, device_id_type=MESH)

    def remote(src, dst, send, recv, target):
        return pltpu.make_async_remote_copy(
            src_ref=src, dst_ref=dst, send_sem=send, recv_sem=recv,
            device_id=target, device_id_type=MESH,
        )

    rate_copies = (
        remote(
            rates.at[:, pl.ds(rows, reach)], rates.at[:, pl.ds(0, reach)],
            rate_send.at[0], rate_recv.at[0], to_next,
        ),
        remote(
            rates.at[:, pl.ds(reach, reach)], rates.at[:, pl.ds(rows + reach, reach)],
            rate_send.at[1], rate_recv.at[1], to_prev,
        ),
    )

    def chunk_of(k):
        return chunks - 1 - k + side * (2 * k - chunks + 1)

    def halo_copies(step, k):
        part = wide.at[step, chunk_of(k)]
        return (
            remote(
                part.at[pl.ds(rows, halo)], part.at[pl.ds(0, halo)],
                halo_send.at[step, k, 0], halo_recv.at[step, k, 0], to_next,
            ),
            remote(
                part.at[pl.ds(halo, halo)], part.at[pl.ds(rows + halo, halo)],
                halo_send.at[step, k, 1], halo_recv.at[step, k, 1], to_prev,
            ),
        )

    def start_two(first, second):
        @pl.when(has_next)
        def _():
            first.start()

        @pl.when(has_prev)
        def _():
            second.start()

    def got_two(first, second):
        @pl.when(has_prev)
        def _():
            first.wait_recv()

        @pl.when(has_next)
        def _():
            second.wait_recv()

    def sent_two(first, second):
        @pl.when(has_next)
        def _():
            first.wait_send()

        @pl.when(has_prev)
        def _():
            second.wait_send()

    def flat(ref, b):
        return ref.at[b].reshape(planes * rows, lanes)

    def across(group, y):
        return pl.ds(group * (SUB * rows) + y, SUB, stride=rows)

    for load in loads[:2]:
        for part in load:
            part.wait()

    def prepare(spans):
        def body(group, carry):
            for y in [y for span in spans for y in span]:
                for b in every:
                    trap = time_step * flat(trap_in, b)[across(group, y), :]
                    release = time_step * flat(rel_in, b)[across(group, y), :]
                    rates[0, reach + y, group, b] = release - trap
                    rates[1, reach + y, group, b] = trap
            return carry

        lax.fori_loop(0, chunks, body, 0)

    prepare((range(reach), range(rows - reach, rows)))

    pl.semaphore_wait(barrier, 1 + has_prev.astype(jnp.int32) + has_next.astype(jnp.int32))
    start_two(*rate_copies)

    for load in loads[2:]:
        for part in load:
            part.wait()

    edge_copies = (
        remote(
            edge_out.at[pl.ds(0, 3)], edge_got.at[pl.ds(0, 3)],
            edge_send.at[0], edge_recv.at[0], partner,
        ),
        remote(edge_out.at[3], edge_got.at[3], edge_send.at[1], edge_recv.at[1], partner),
    )

    lane = lax.broadcasted_iota(jnp.int32, (SUB, lanes), 1)
    lane_first, lane_last = lane == 0, lane == lanes - 1

    def substep(inner, span, read, group, write):
        start = span[0]

        def clean(y, value):
            if y < 0:
                return jnp.where(has_prev, value, 0.0)
            if y >= rows:
                return jnp.where(has_next, value, 0.0)
            return value

        def fetch(y):
            got = [read(y, b) for b in every]
            return [clean(y, v) for v in got] if inner == 0 else got

        window = [fetch(start - 1), fetch(start)]
        for y in span:
            window.append(fetch(y + 1))
            above, center, below = window[-3:]
            window = window[-2:]
            right = [pltpu.roll(v, 1, axis=1) for v in center]
            left = [pltpu.roll(v, lanes - 1, axis=1) for v in center]
            for b in every:
                c = center[b]
                lower = jnp.where(lane_first, right[b - 1] if b > 0 else c, right[b])
                upper = jnp.where(lane_last, left[b + 1] if b < blocks - 1 else c, left[b])
                value = (
                    (1.0 - 2.0 * y_weight - 2.0 * z_weight) * c
                    + y_weight * (above[b] + below[b])
                    + z_weight * (lower + upper)
                    + (
                        rates[0, reach + y, group, b]
                        + rates[1, reach + y, group, b] * inverse(1.0 + c * c)
                    )
                )
                write(y, b, clean(y, value))

    def plane(ref, x):
        return [ref[b, x] for b in every]

    for step in range(STEPS):
        def position(i):
            return i + side * (planes - 1 - 2 * i)

        right = plane(c_in, position(0))
        if step == 0:
            main = [jnp.ones_like(v) for v in right]
        for i in range(planes - 1):
            if step == 0:
                face = plane(f_in, i + side * (planes - 2 - 2 * i))
                inv = [inverse(main[b] + face[b]) for b in every]
                ratio = [face[b] * inv[b] for b in every]
                for b in every:
                    factor[i, b] = ratio[b]
                    scale[i, b] = inv[b]
                main = [1.0 + ratio[b] * main[b] for b in every]
            else:
                ratio = [factor[i, b] for b in every]
                inv = [scale[i, b] for b in every]
            following = plane(c_in, position(i + 1))
            for b in every:
                partial[i, b] = right[b] * inv[b]
            right = [following[b] + ratio[b] * right[b] for b in every]
        if step == 0:
            for b in every:
                edge_out[0, b] = right[b]
                edge_out[1, b] = main[b]
                edge_out[2, b] = f_in[b, planes - 1]
            edge_copies[0].start()
            prepare((range(reach, rows - reach),))
            edge_copies[0].wait_recv()
            value = []
            for b in every:
                other = edge_got[1, b]
                face = jnp.where(side == 0, f_in[b, planes - 1], edge_got[2, b])
                inv = inverse(main[b] * other + face * (main[b] + other))
                own_weight = (other + face) * inv
                other_weight = face * inv
                value.append(own_weight * right[b] + other_weight * edge_got[0, b])
                edge_out[4, b] = own_weight
                edge_out[5, b] = other_weight
        else:
            for b in every:
                edge_out[3, b] = right[b]
            edge_copies[1].start()
            edge_copies[1].wait_recv()
            value = [
                edge_out[4, b] * right[b] + edge_out[5, b] * edge_got[3, b] for b in every
            ]
        for k in range(chunks):
            for i in reversed(range((chunks - 1 - k) * SUB, (chunks - k) * SUB)):
                if i < planes - 1:
                    value = [partial[i, b] + factor[i, b] * value[b] for b in every]
                for b in every:
                    solved[b, position(i)] = value[b]
            group = chunk_of(k)
            for y in range(rows):
                for b in every:
                    wide[step, group, halo + y, b] = flat(solved, b)[across(group, y), :]
            start_two(*halo_copies(step, k))

        def run(group, spans_of, step=step):
            def first(y, b):
                return wide[step, group, halo + y, b]

            def level(inner):
                return lambda y, b: levels[inner, group, halo + y, b]

            def keep(inner):
                def put(y, b, value):
                    levels[inner, group, halo + y, b] = value
                return put

            def last(y, b, value):
                flat(c_in, b)[across(group, y), :] = value

            for inner in range(SUBSTEPS):
                for span in spans_of(inner):
                    substep(
                        inner, span,
                        first if inner == 0 else level(inner - 1),
                        group,
                        last if inner == SUBSTEPS - 1 else keep(inner),
                    )

        def inside(k, carry):
            run(chunk_of(k), lambda inner: (range(inner + 1, rows - 1 - inner),))
            return carry

        def finish(k, carry, step=step):
            group = chunk_of(k)
            got_two(*halo_copies(step, k))
            run(group, lambda inner: (
                range(inner - reach, inner + 1),
                range(rows - 1 - inner, rows + reach - inner),
            ))
            if step == STEPS - 1:
                for n in range(SUB):
                    x = group * SUB + n
                    for b in every:
                        out[x, :, b * lanes:(b + 1) * lanes] = c_in[b, x]
            return carry

        lax.fori_loop(0, chunks, inside, 0)
        if step == 0:
            got_two(*rate_copies)
        lax.fori_loop(0, chunks, finish, 0)

    for copy in edge_copies:
        copy.wait_send()
    sent_two(*rate_copies)
    for step in range(STEPS):
        for k in range(chunks):
            sent_two(*halo_copies(step, k))


def fused(concentration, face_conductance, release, trap_rate):
    planes, rows, depth = concentration.shape
    blocks, chunks = depth // LANES, planes // SUB
    block = pltpu.VMEM((blocks, planes, rows, LANES), jnp.float32)
    kept = pltpu.VMEM((planes, blocks, rows, LANES), jnp.float32)
    edge = pltpu.VMEM((6, blocks, rows, LANES), jnp.float32)
    stage = pltpu.VMEM(
        (SUBSTEPS - 1, chunks, rows + 2 * SUBSTEPS, blocks, SUB, LANES), jnp.float32
    )
    parts = pl.pallas_call(
        kernel,
        out_shape=pltpu.VMEM((planes, rows, depth), jnp.float32),
        in_specs=[pl.BlockSpec(memory_space=pl.ANY)] * 4,
        out_specs=pl.BlockSpec(memory_space=pltpu.VMEM),
        scratch_shapes=[block] * 4 + [kept] * 3 + [block] + [
            pltpu.VMEM(
                (2, rows + 2 * (SUBSTEPS - 1), chunks, blocks, SUB, LANES), jnp.float32
            ),
            pltpu.VMEM(
                (STEPS, chunks, rows + 2 * SUBSTEPS, blocks, SUB, LANES), jnp.float32
            ),
            stage, edge, edge,
            pltpu.SemaphoreType.DMA((4, blocks)),
            pltpu.SemaphoreType.DMA((2,)),
            pltpu.SemaphoreType.DMA((2,)),
            pltpu.SemaphoreType.DMA((2,)),
            pltpu.SemaphoreType.DMA((2,)),
            pltpu.SemaphoreType.DMA((STEPS, chunks, 2)),
            pltpu.SemaphoreType.DMA((STEPS, chunks, 2)),
        ],
        compiler_params=pltpu.CompilerParams(
            collective_id=0, has_side_effects=True, vmem_limit_bytes=VMEM_LIMIT
        ),
    )(concentration, face_conductance, release, trap_rate)
    return parts


def solution(mesh):
    placed = (P("gx", "gy", None), P("gx", "gy", None), P("gx", "gy", None), P("gx", "gy", None))

    def body(concentration, *rest):
        planes, rows, depth = concentration.shape
        fits = (
            mesh.shape["gx"] == 2
            and planes % SUB == 0
            and rows >= 2 * SUBSTEPS
            and rows % SUB == 0
            and depth % LANES == 0
        )
        return (fused if fits else local)(concentration, *rest)

    return jax.shard_map(
        body, mesh=mesh, in_specs=placed, out_specs=P("gx", "gy", None), check_vma=False
    )
```
